256 devices in a mesh: wide: 32 (over x, z), blk: 8 (over y, core).
Axes of the slice: x: 4, y: 4, z: 8, core: 2. Of those that a mesh axis runs over, the one named last changes fastest.
Arguments:
- amplitudes: bfloat16 [32, 32, 32, 4096], P('blk', 'wide'), may hold values from -6 to 6
- integrals: bfloat16 [32, 2, 2048, 4096], P('wide', None, 'blk'), may hold values from -0.09375 to 0.09375
- owner: int32 [32], replicated, may hold values from 0 to 31, each once
- targets: int32 [32, 2], replicated, may hold values from 0 to 31, all different within a row
- counts: int32 [32], replicated, may hold values from 1 to 2, 48 in all
Outputs:
- ladder: bfloat16 [32, 32, 32, 2048], P(None, 'blk', 'wide')
The draws below stay inside these ranges and needn't reach their ends.
Inputs may be any that keep to these rules, and one draw needn't show every extreme that they name: Each contracted tile has its own owner slot. `targets`: the output tiles of one contracted tile are distinct, and every output tile is named by some contracted tile. The counts sum to 48 and one of them is 2.
All inputs are finite; a program needn't handle non-finite values.
Results may differ from the reference program's by a relative error of at most 0.0044.
Values may be sent and summed in bfloat16 or wider, within the bound.
A program may use at most 128 MiB of HBM per device.

```python
import math
import jax
import jax.numpy as jnp
import numpy as np
from jax import lax

TW = 4096
NI = 32
NJ = 32
AB = 2048
KMAX = 2
NT = 32
NP = 32


def shard_levels(key, shape, pieces, smallest, top_value):
    factor_of, own = 1.0, jax.random.fold_in(key, 6)
    for position, shards_of in pieces:
        steps = jnp.exp(jax.random.uniform(jax.random.fold_in(own, position), (shards_of,), jnp.float32, smallest / len(pieces), top_value / len(pieces)))
        factor_of = factor_of * jnp.repeat(steps, shape[position] // shards_of).reshape([-1 if axis == position else 1 for axis in range(len(shape))])
    return factor_of


def distinct(key, rows, count, top, lift):
    sequence = jax.random.permutation(jax.random.fold_in(key, 1), count)
    pull = sequence
    for power in range(3):
        pull = pull * pull // count
    pull = pull * lift // count
    chance = jax.random.randint(jax.random.fold_in(key, 2), (rows, count), 0, 4096) + pull
    fixed_rows = jax.random.permutation(jax.random.fold_in(key, 3), rows)[jnp.arange(count) % rows]
    chance = jnp.where(jnp.arange(rows)[:, None] == fixed_rows[None, :], 1 << 14, chance)
    score = chance * count + jnp.arange(count)
    return lax.top_k(score.astype(jnp.int32), top)[1].astype(jnp.int32)


def profile(count, total, most, slope):
    weights = [(1 << 20) // math.isqrt(rank ** slope) + 1 for rank in range(2, count + 1)]
    rest, holding = total - most - (count - 1), [1] * (count - 1)
    while rest > 0:
        movable = [i for i in range(count - 1) if holding[i] < most]
        mass, left = sum([weights[i] for i in movable]), rest
        for i in movable:
            more = min(most - holding[i], max(1, left * weights[i] // mass), rest)
            holding[i] = holding[i] + more
            rest = rest - more
    return np.array([most] + holding)


def uneven(rng, amount, total, most, lean):
    if amount == 2:
        one = jax.random.randint(rng, (), max(1, total - most), min(most, total - 1) + 1)
        return jnp.stack([one, total - one])
    sizes = jnp.asarray(profile(amount, total, most, lean), jnp.int32)
    couples = (amount - 1) // 2
    source_of, sink = sizes[1:1 + 2 * couples:2], sizes[2:2 + 2 * couples:2]
    slack = jnp.minimum(source_of - 1, most - sink)
    shifted = jax.random.randint(jax.random.fold_in(rng, 1), (couples,), 0, 1 << 20) % (slack + 1)
    sizes = sizes.at[1:1 + 2 * couples:2].set(source_of - shifted).at[2:2 + 2 * couples:2].set(sink + shifted)
    return sizes[jax.random.permutation(jax.random.fold_in(rng, 2), amount)]


def gaussian(own_key, dims, spread, bound, split=(), held_as=jnp.bfloat16):
    drawn = spread * jax.random.normal(own_key, dims, jnp.float32)
    if split:
        drawn = drawn * shard_levels(own_key, dims, split, -0.22, 0.18)
    return jnp.clip(drawn, -bound, bound).astype(held_as)


def setup_inputs(seed: int = 0) -> dict:
    keys = jax.random.split(jax.random.key(seed), 6)
    amplitudes = gaussian(keys[0], (NI, NJ, NT, TW), 1.0, 6.0, ((0, 8), (1, 32)))
    integrals = gaussian(keys[1], (NT, KMAX, AB, TW), TW ** -0.5, 0.09375, ((0, 32), (2, 8)))
    owner = jax.random.permutation(keys[2], NT).astype(jnp.int32)
    targets = distinct(keys[3], NT, NP, KMAX, 512)
    counts = uneven(keys[4], NT, 3 * NT // 2, KMAX, 0).astype(jnp.int32)
    return dict(amplitudes=amplitudes, integrals=integrals, owner=owner, targets=targets, counts=counts)


def reference(amplitudes, integrals, owner, targets, counts):
    pair_count = NI * NJ

    def accumulate(running, tile_index):
        amp_tile = lax.dynamic_index_in_dim(amplitudes, tile_index, 2, keepdims=False)
        amp_tile = amp_tile.reshape(pair_count, TW).astype(jnp.float32)
        integral_block = lax.dynamic_index_in_dim(integrals, owner[tile_index], 0, keepdims=False).astype(jnp.float32)
        for slot_index in range(KMAX):
            product = jnp.dot(amp_tile, integral_block[slot_index].T, precision=lax.Precision.HIGHEST)
            rounded = lax.optimization_barrier(product.astype(jnp.bfloat16)).astype(jnp.float32)
            kept_flag = (slot_index < counts[tile_index]).astype(jnp.float32)
            running = running.at[targets[tile_index, slot_index]].add(rounded * kept_flag)
        return running, None

    start_sum = jnp.zeros((NP, pair_count, AB), jnp.float32)
    running, unused = lax.scan(accumulate, start_sum, jnp.arange(NT, dtype=jnp.int32))
    return running.reshape(NP, NI, NJ, AB).astype(jnp.bfloat16)
```

```python
import jax
import jax.numpy as jnp
from jax import lax
from jax.sharding import PartitionSpec as P


def body(amplitudes, integrals, owner, targets, counts):
    wide_count = lax.axis_size("wide")
    blk_count = lax.axis_size("blk")
    my_index = lax.axis_index("wide")
    tile_ids = jnp.arange(owner.shape[0], dtype=jnp.int32)
    holder = jnp.sum(jnp.where(owner[None, :] == tile_ids[:, None], tile_ids[None, :], 0), axis=1)
    ni, _, nt, width = amplitudes.shape
    ordered = jnp.take(amplitudes.reshape(ni, nt, width).transpose(1, 0, 2), holder, axis=0)
    my_tile = lax.all_to_all(ordered, "wide", split_axis=0, concat_axis=0, tiled=True)
    rows = lax.all_gather(my_tile.reshape(wide_count * ni, width), "blk", axis=0, tiled=True)
    my_holder = lax.dynamic_index_in_dim(holder, my_index, 0, keepdims=False)
    my_count = lax.dynamic_index_in_dim(counts, my_holder, 0, keepdims=False)
    slot_ids = jnp.arange(targets.shape[1], dtype=jnp.int32)
    live_slots = (slot_ids < my_count).astype(jnp.float32)
    value = jnp.einsum("rc,kac->rka", rows, integrals[0], preferred_element_type=jnp.float32)
    shaped = (value * live_slots[None, :, None]).astype(jnp.bfloat16)
    nk, ab = shaped.shape[1:]
    shaped = shaped.reshape(blk_count, wide_count, ni, nk, ab).transpose(1, 0, 2, 3, 4)
    shaped = shaped.reshape(wide_count * blk_count, ni, nk, ab)
    received = lax.all_to_all(shaped, ("wide", "blk"), split_axis=0, concat_axis=0, tiled=True)
    received = received.reshape(wide_count, blk_count, ni, nk, ab)
    slot_targets = jnp.take(targets, holder, axis=0)
    window_ids = jnp.arange(wide_count, dtype=jnp.int32)
    selector = (slot_targets[None] == window_ids[:, None, None]).astype(jnp.bfloat16)
    ladder = jnp.einsum("pwk,wbika->piba", selector, received, preferred_element_type=jnp.float32)
    ladder = ladder.astype(jnp.bfloat16)
    return ladder.reshape(wide_count, ni, 1, blk_count * ab)


def solution(mesh):
    placed = (P("blk", "wide", None, None), P("wide", None, "blk", None), P(), P(), P())
    return jax.shard_map(
        body, mesh=mesh, in_specs=placed, out_specs=P(None, "blk", "wide", None), check_vma=False
    )
```

```python
import functools
import jax
import jax.numpy as jnp
from jax import lax
from jax.experimental import pallas as pl
from jax.experimental.pallas import tpu as pltpu
from jax.sharding import PartitionSpec as P

MESH = pl.DeviceIdType.MESH
NX, NY, NZ = 4, 4, 8
NW = NX * NZ
NI = 4
ROWS = NW * NI
NT_DIMS = (((1,), (1,)), ((), ()))


def kernel(tab, amps, ints, out, stage, got, rows, held, made, back,
           arrive, from_up, from_down, far, home, local, sent, swap):
    w, b = lax.axis_index("wide"), lax.axis_index("blk")
    x, z = w // NZ, w % NZ
    y, c = b // 2, b % 2

    def wide_at(step, sign):
        dx, dz = step // NZ, step % NZ
        return ((x + NX + sign * dx) % NX) * NZ + (z + NZ + sign * dz) % NZ

    def blk_at(dy):
        return ((y + dy) % NY) * 2 + c

    def remote(src, dst, send, recv, device):
        return pltpu.make_async_remote_copy(
            src_ref=src, dst_ref=dst, send_sem=send, recv_sem=recv,
            device_id=device, device_id_type=MESH)

    partner = (w, y * 2 + 1 - c)

    barrier = pltpu.get_barrier_semaphore()
    pl.semaphore_signal(barrier, inc=1, device_id=partner, device_id_type=MESH)
    for dy in range(NY):
        @pl.loop(1 if dy == 0 else 0, NW)
        def _(step):
            pl.semaphore_signal(barrier, inc=1, device_id=(wide_at(step, 1), blk_at(dy)), device_id_type=MESH)

    own = pltpu.make_async_copy(ints, held.at[c], local.at[0])
    own.start()

    row = lax.broadcasted_iota(jnp.int32, (ROWS, ROWS), 0)
    col = lax.broadcasted_iota(jnp.int32, (ROWS, ROWS), 1)
    slot = jnp.broadcast_to(tab[2:3, :], (ROWS, ROWS))
    order = jnp.where((slot == row // NI) & (row % NI == col // NW), 1.0, 0.0).astype(jnp.bfloat16)
    width = amps.shape[2]
    for j in range(4):
        lanes = slice(j * width // 4, (j + 1) * width // 4)
        piece = amps[:, :, lanes].reshape(ROWS, width // 4)
        value = jnp.dot(order, piece, preferred_element_type=jnp.float32).astype(jnp.bfloat16)
        stage[:, :, lanes] = value.reshape(NW, NI, width // 4)

    pl.semaphore_wait(barrier, NW * NY)

    @pl.loop(1, NW)
    def _(step):
        to = wide_at(step, 1)
        remote(stage.at[to], got.at[0, step], sent.at[0], arrive.at[step], (to, b)).start()

    mine = pltpu.make_async_copy(stage.at[w], got.at[0, 0], arrive.at[0])
    mine.start()
    exchange = remote(ints, held.at[c], swap.at[0], swap.at[1], partner)
    exchange.start()

    up, down = (w, blk_at(1)), (w, blk_at(NY - 1))
    GROUP = 4

    def lay(part, group):
        first = pl.multiple_of(group * GROUP, GROUP)
        piece = got[part, pl.ds(first, GROUP)].reshape(GROUP * NI, width)
        rows[part, pl.ds(pl.multiple_of(group * GROUP * NI, GROUP * NI), GROUP * NI), :] = piece

    @pl.loop(0, NW // GROUP)
    def _(group):
        for j in range(GROUP):
            step = group * GROUP + j
            chunk = got.at[0, step]
            pltpu.make_async_copy(chunk, chunk, arrive.at[step]).wait()
            remote(chunk, got.at[3, step], sent.at[1], from_down.at[step], up).start()
            remote(chunk, got.at[1, step], sent.at[2], from_up.at[step], down).start()
        lay(0, group)

    own.wait()
    exchange.wait_recv()

    def contract(part):
        for cc in range(2):
            for k in range(2):
                value = lax.dot_general(rows[part], held[cc, k], NT_DIMS, preferred_element_type=jnp.float32)
                n = value.shape[1]
                lanes = slice((cc * 2 + k) * n, (cc * 2 + k + 1) * n)
                made[part, :, :, lanes] = value.astype(jnp.bfloat16).reshape(NW, NI, n)

    def give(part):
        to_blk = blk_at(part)

        @pl.loop(1 if part == 0 else 0, NW)
        def _(step):
            remote(made.at[part, step], back.at[y, w], sent.at[5], home.at[part], (wide_at(step, -1), to_blk)).start()

    contract(0)
    pltpu.make_async_copy(made.at[0, 0], back.at[y, w], home.at[0]).start()
    give(0)

    @pl.loop(0, NW // GROUP)
    def _(group):
        for j in range(GROUP):
            step = group * GROUP + j
            low, high = got.at[3, step], got.at[1, step]
            pltpu.make_async_copy(low, low, from_down.at[step]).wait()
            pltpu.make_async_copy(high, high, from_up.at[step]).wait()
            if j % 2 == 0:
                remote(low, got.at[2, step], sent.at[3], far.at[step], up).start()
            else:
                remote(high, got.at[2, step], sent.at[4], far.at[step], down).start()
        lay(3, group)
        lay(1, group)

    contract(3)
    give(3)
    contract(1)
    give(1)

    @pl.loop(0, NW // GROUP)
    def _(group):
        for j in range(GROUP):
            step = group * GROUP + j
            chunk = got.at[2, step]
            pltpu.make_async_copy(chunk, chunk, far.at[step]).wait()
        lay(2, group)

    contract(2)
    give(2)

    pick = []
    for k in range(2):
        target = jnp.broadcast_to(tab[k:k + 1, :], (ROWS, ROWS))
        pick.append(jnp.where((target == row // NI) & (row % NI == col % NI), 1.0, 0.0).astype(jnp.bfloat16))
    for part in (0, 3, 1, 2):
        origin = (y + NY - part) % NY
        block = back.at[origin]
        pltpu.make_async_copy(block, block, home.at[part]).wait()
        piece = back[origin].reshape(ROWS, back.shape[3])
        n = piece.shape[1] // 4
        for cc in range(2):
            total = jnp.dot(pick[0], piece[:, 2 * cc * n:(2 * cc + 1) * n], preferred_element_type=jnp.float32)
            total += jnp.dot(pick[1], piece[:, (2 * cc + 1) * n:(2 * cc + 2) * n], preferred_element_type=jnp.float32)
            lanes = pl.ds(pl.multiple_of((origin * 2 + cc) * n, n), n)
            out[:, :, lanes] = total.astype(jnp.bfloat16).reshape(NW, NI, n)

    def drain(ref, sem):
        pltpu.make_async_copy(ref, ref, sem).wait()

    drain(stage.at[pl.ds(0, NW - 1)], sent.at[0])
    drain(got.at[0], sent.at[1])
    drain(got.at[0], sent.at[2])
    drain(got.at[2, pl.ds(0, NW // 2)], sent.at[3])
    drain(got.at[2, pl.ds(0, NW // 2)], sent.at[4])
    for part in range(NY):
        if part:
            drain(made.at[part], sent.at[5])
        else:
            drain(made.at[part, pl.ds(0, NW - 1)], sent.at[5])
    exchange.wait_send()


def table(owner, targets, counts):
    shape = (8, ROWS, NW)
    r, m, q = (lax.broadcasted_iota(jnp.int32, shape, axis) for axis in range(3))
    second = jnp.where(counts > 1, targets[:, 1], -1)[None, None]
    first = jnp.where(counts > 0, targets[:, 0], -1)[None, None]
    target = jnp.where(r == 0, first, second)
    owners = owner[None, None]
    value = jnp.where(r < 2, jnp.where(owners == m // NI, target, 0), jnp.where(q == m % NW, owners, 0))
    return jnp.sum(value, axis=2)


def body(amplitudes, integrals, owner, targets, counts):
    amps, ints = amplitudes[:, 0], integrals[0]
    width = amps.shape[2]
    pairs = ints.shape[1]
    vmem = pl.BlockSpec(memory_space=pltpu.VMEM)
    dma = pltpu.SemaphoreType.DMA
    out = pl.pallas_call(
        kernel,
        out_shape=jax.ShapeDtypeStruct((NW, NI, 2 * NY * pairs), jnp.bfloat16),
        in_specs=[vmem, vmem, pl.BlockSpec(memory_space=pl.ANY)],
        out_specs=vmem,
        scratch_shapes=[
            pltpu.VMEM((NW, NI, width), jnp.bfloat16),
            pltpu.VMEM((NY, NW, NI, width), jnp.bfloat16),
            pltpu.VMEM((NY, ROWS, width), jnp.bfloat16),
            pltpu.VMEM((2, 2, pairs, width), jnp.bfloat16),
            pltpu.VMEM((NY, NW, NI, 4 * pairs), jnp.bfloat16),
            pltpu.VMEM((NY, NW, NI, 4 * pairs), jnp.bfloat16),
            dma((NW,)), dma((NW,)), dma((NW,)), dma((NW,)), dma((NY,)), dma((1,)), dma((6,)), dma((2,)),
        ],
        compiler_params=pltpu.CompilerParams(
            collective_id=0, has_side_effects=True, vmem_limit_bytes=48 << 20),
        name="ladder",
    )(table(owner, targets, counts), amps, ints)
    return out[:, :, None, :]


def solution(mesh):
    placed = (P("blk", "wide", None, None), P("wide", None, "blk", None), P(), P(), P())
    return jax.shard_map(
        body, mesh=mesh, in_specs=placed, out_specs=P(None, "blk", "wide", None), check_vma=False
    )
```

```python
import functools
import jax
import jax.numpy as jnp
from jax import lax
from jax.experimental import pallas as pl
from jax.experimental.pallas import tpu as pltpu
from jax.sharding import PartitionSpec as P

MESH = pl.DeviceIdType.MESH
NX, NY, NZ = 4, 4, 8
NW = NX * NZ
NI = 4
ROWS = NW * NI
GROUP = 4
GROUPS = NW // GROUP
HALF = NW // 2
PLACE = (0, 2, 3, 1)
NT_DIMS = (((1,), (1,)), ((), ()))


def kernel(owner_hbm, targets_hbm, counts_hbm, amps_hbm, ints, out,
           owner, targets, counts, amps, stage, got, rows, held, made, back,
           arrive, from_up, from_down, far, home, local, sent, swap):
    w, b = lax.axis_index("wide"), lax.axis_index("blk")
    x, z = w // NZ, w % NZ
    y, c = b // 2, b % 2

    def offset(step):
        iz, ix = step // NX, step % NX
        dz = NZ // 2 + (iz + 1) // 2 * (1 - 2 * (iz % 2))
        dx = NX // 2 + (ix + 1) // 2 * (1 - 2 * (ix % 2))
        return dx, dz

    def wide_at(step, sign):
        dx, dz = offset(step)
        return ((x + NX + sign * dx) % NX) * NZ + (z + NZ + sign * dz) % NZ

    def blk_at(dy):
        return ((y + dy) % NY) * 2 + c

    def remote(src, dst, send, recv, device):
        return pltpu.make_async_remote_copy(
            src_ref=src, dst_ref=dst, send_sem=send, recv_sem=recv,
            device_id=device, device_id_type=MESH)

    def await_bytes(ref, sem):
        pltpu.make_async_copy(ref, ref, sem).wait()

    partner = (w, y * 2 + 1 - c)

    loads = [pltpu.make_async_copy(src, dst, local.at[n]) for n, (src, dst) in enumerate((
        (amps_hbm, amps), (owner_hbm, owner), (targets_hbm, targets), (counts_hbm, counts), (ints, held.at[c])))]
    for load in loads:
        load.start()

    barrier = pltpu.get_barrier_semaphore()
    pl.semaphore_signal(barrier, inc=1, device_id=partner, device_id_type=MESH)

    @pl.loop(0, NW - 1)
    def _(step):
        there = wide_at(step, 1)
        for dy in range(NY):
            pl.semaphore_signal(barrier, inc=1, device_id=(there, blk_at(dy)), device_id_type=MESH)

    for dy in range(1, NY):
        pl.semaphore_signal(barrier, inc=1, device_id=(w, blk_at(dy)), device_id_type=MESH)

    for load in loads[:4]:
        load.wait()
    row = lax.broadcasted_iota(jnp.int32, (ROWS, ROWS), 0)
    col = lax.broadcasted_iota(jnp.int32, (ROWS, ROWS), 1)
    same = row % NI == col // NW

    def spread(value):
        return jnp.broadcast_to(jnp.concatenate([value] * NI, axis=1), (ROWS, ROWS))

    def one_hot(value):
        return jnp.where((spread(value) == row // NI) & same, 1.0, 0.0).astype(jnp.bfloat16)

    order = one_hot(owner[...])
    width = amps.shape[2]
    for j in range(4):
        lanes = slice(j * width // 4, (j + 1) * width // 4)
        piece = amps[:, :, lanes].reshape(ROWS, width // 4)
        value = jnp.dot(order, piece, preferred_element_type=jnp.float32).astype(jnp.bfloat16)
        stage[:, :, lanes] = value.reshape(NW, NI, width // 4)

    pl.semaphore_wait(barrier, NW * NY)

    mine = pltpu.make_async_copy(stage.at[w], got.at[0, NW - 1], arrive.at[NW - 1])
    mine.start()

    @pl.loop(0, NW - 1)
    def _(step):
        to = wide_at(step, 1)
        remote(stage.at[to], got.at[0, step], sent.at[0], arrive.at[step], (to, b)).start()

    exchange = remote(ints, held.at[c], swap.at[0], swap.at[1], partner)
    exchange.start()

    pick = []
    for k in range(2):
        live = jnp.where(counts[...] > k, targets[k:k + 1, :], -1)
        chosen = lax.dot_general(one_hot(live), order, NT_DIMS, preferred_element_type=jnp.float32)
        pick.append(chosen.astype(jnp.bfloat16))

    up, down = (w, blk_at(1)), (w, blk_at(NY - 1))

    def lay(part, group):
        first = pl.multiple_of(group * GROUP, GROUP)
        piece = got[part, pl.ds(first, GROUP)].reshape(GROUP * NI, width)
        place = (group // 4 * NY + PLACE[part]) * 64 + group % 4 * 16
        rows[pl.ds(pl.multiple_of(place, 16), 16), :] = piece

    def forward(group):
        for j in range(GROUP):
            step = group * GROUP + j
            chunk = got.at[0, step]
            await_bytes(chunk, arrive.at[step])
            remote(chunk, got.at[3, step], sent.at[1], from_down.at[step], up).start()
            remote(chunk, got.at[1, step], sent.at[2], from_up.at[step], down).start()
        lay(0, group)

    def relay(group):
        for j in range(GROUP):
            step = group * GROUP + j
            low, high = got.at[3, step], got.at[1, step]
            await_bytes(low, from_down.at[step])
            await_bytes(high, from_up.at[step])
            if j % 2 == 0:
                remote(low, got.at[2, step], sent.at[3], far.at[step], up).start()
            else:
                remote(high, got.at[2, step], sent.at[4], far.at[step], down).start()
        lay(3, group)
        lay(1, group)

    def finish(group):
        for j in range(GROUP):
            step = group * GROUP + j
            await_bytes(got.at[2, step], far.at[step])
        lay(2, group)

    def contract(first, count):
        for cc in range(2):
            for k in range(2):
                value = lax.dot_general(rows[first * 64:(first + count) * 64, :], held[cc, k], NT_DIMS,
                                        preferred_element_type=jnp.float32)
                n = value.shape[1]
                lanes = slice((cc * 2 + k) * n, (cc * 2 + k + 1) * n)
                made[first * HALF:(first + count) * HALF, :, lanes] = value.astype(jnp.bfloat16).reshape(count * HALF, NI, n)

    def give(part, half):
        to_blk = blk_at(part)
        base = (half * NY + PLACE[part]) * HALF

        @pl.loop(0, HALF - 1 if part == 0 and half == 1 else HALF)
        def _(n):
            remote(made.at[base + n], back.at[y, w], sent.at[5], home.at[part],
                   (wide_at(half * HALF + n, -1), to_blk)).start()

        if part == 0 and half == 1:
            pltpu.make_async_copy(made.at[base + HALF - 1], back.at[y, w], home.at[0]).start()

    @pl.loop(0, 2)
    def _(group):
        forward(group)

    @pl.loop(2, 4)
    def _(group):
        forward(group)
        relay(group - 2)

    loads[4].wait()
    exchange.wait_recv()
    contract(0, 1)
    give(0, 0)

    @pl.loop(4, 6)
    def _(group):
        forward(group)
        relay(group - 2)
        finish(group - 4)

    contract(1, 2)
    give(3, 0)
    give(1, 0)

    @pl.loop(6, 8)
    def _(group):
        forward(group)
        relay(group - 2)
        finish(group - 4)

    contract(3, 2)
    give(2, 0)
    give(0, 1)

    @pl.loop(6, 8)
    def _(group):
        relay(group)

    contract(5, 2)
    give(3, 1)
    give(1, 1)

    @pl.loop(4, 8)
    def _(group):
        finish(group)

    contract(7, 1)
    give(2, 1)

    for part in (0, 3, 1, 2):
        origin = (y + NY - part) % NY
        await_bytes(back.at[origin], home.at[part])
        piece = back[origin].reshape(ROWS, back.shape[3])
        n = piece.shape[1] // 4
        for cc in range(2):
            total = jnp.dot(pick[0], piece[:, 2 * cc * n:(2 * cc + 1) * n], preferred_element_type=jnp.float32)
            total += jnp.dot(pick[1], piece[:, (2 * cc + 1) * n:(2 * cc + 2) * n], preferred_element_type=jnp.float32)
            lanes = pl.ds(pl.multiple_of((origin * 2 + cc) * n, n), n)
            out[:, :, lanes] = total.astype(jnp.bfloat16).reshape(NW, NI, n)

    await_bytes(stage.at[pl.ds(0, NW - 1)], sent.at[0])
    await_bytes(got.at[0], sent.at[1])
    await_bytes(got.at[0], sent.at[2])
    await_bytes(got.at[2, pl.ds(0, HALF)], sent.at[3])
    await_bytes(got.at[2, pl.ds(0, HALF)], sent.at[4])
    await_bytes(made.at[pl.ds(0, 8 * HALF - 1)], sent.at[5])
    exchange.wait_send()


def body(amplitudes, integrals, owner, targets, counts):
    amps, ints = amplitudes[:, 0], integrals[0]
    width = amps.shape[2]
    pairs = ints.shape[1]
    dma = pltpu.SemaphoreType.DMA
    out = pl.pallas_call(
        kernel,
        out_shape=jax.ShapeDtypeStruct((NW, NI, 2 * NY * pairs), jnp.bfloat16),
        in_specs=[pl.BlockSpec(memory_space=pl.ANY)] * 5,
        out_specs=pl.BlockSpec(memory_space=pltpu.VMEM),
        scratch_shapes=[
            pltpu.VMEM((1, NW), jnp.int32),
            pltpu.VMEM((2, NW), jnp.int32),
            pltpu.VMEM((1, NW), jnp.int32),
            pltpu.VMEM((NI, NW, width), jnp.bfloat16),
            pltpu.VMEM((NW, NI, width), jnp.bfloat16),
            pltpu.VMEM((NY, NW, NI, width), jnp.bfloat16),
            pltpu.VMEM((NY * ROWS, width), jnp.bfloat16),
            pltpu.VMEM((2, 2, pairs, width), jnp.bfloat16),
            pltpu.VMEM((NY * NW, NI, 4 * pairs), jnp.bfloat16),
            pltpu.VMEM((NY, NW, NI, 4 * pairs), jnp.bfloat16),
            dma((NW,)), dma((NW,)), dma((NW,)), dma((NW,)), dma((NY,)), dma((5,)), dma((6,)), dma((2,)),
        ],
        compiler_params=pltpu.CompilerParams(
            collective_id=0, has_side_effects=True, vmem_limit_bytes=60 << 20),
        name="ladder",
    )(owner[None], targets.T, counts[None], amps, ints)
    return out[:, :, None, :]


def solution(mesh):
    placed = (P("blk", "wide", None, None), P("wide", None, "blk", None), P(), P(), P())
    return jax.shard_map(
        body, mesh=mesh, in_specs=placed, out_specs=P(None, "blk", "wide", None), check_vma=False
    )
```

```python
import functools
import jax
import jax.numpy as jnp
from jax import lax
from jax.experimental import pallas as pl
from jax.experimental.pallas import tpu as pltpu
from jax.sharding import PartitionSpec as P

MESH = pl.DeviceIdType.MESH
NX, NY, NZ = 4, 4, 8
NW = NX * NZ
NI = 4
ROWS = NW * NI
GROUP = 4
GROUPS = NW // GROUP
HALF = NW // 2
DZ = (0, 1, 7, 4, 3, 5, 2, 6)
PLACE = (0, 2, 3, 1)
NT_DIMS = (((1,), (1,)), ((), ()))


def kernel(owner_hbm, targets_hbm, counts_hbm, amps_hbm, ints, out,
           owner, targets, counts, amps, stage, got, rows, held, turned, made, back,
           arrive, from_up, from_down, far, home, local, sent, swap):
    w, b = lax.axis_index("wide"), lax.axis_index("blk")
    y, c = b // 2, b % 2
    xs = [lax.rem(w // NZ + d, NX) * NZ for d in range(NX)]
    zs = [lax.rem(w % NZ + d, NZ) for d in range(NZ)]
    blks = [lax.rem(y + d, NY) * 2 + c for d in range(NY)]

    def wide_at(step, sign):
        dz, dx = DZ[step // NX], step % NX
        return xs[sign * dx % NX] + zs[sign * dz % NZ]

    def remote(src, dst, send, recv, device):
        return pltpu.make_async_remote_copy(
            src_ref=src, dst_ref=dst, send_sem=send, recv_sem=recv,
            device_id=device, device_id_type=MESH)

    def await_bytes(ref, sem):
        pltpu.make_async_copy(ref, ref, sem).wait()

    partner = (w, y * 2 + 1 - c)

    loads = [pltpu.make_async_copy(src, dst, local.at[n]) for n, (src, dst) in enumerate((
        (amps_hbm, amps), (owner_hbm, owner), (targets_hbm, targets), (counts_hbm, counts), (ints, held.at[c])))]
    for load in loads:
        load.start()

    barrier = pltpu.get_barrier_semaphore()
    pl.semaphore_signal(barrier, inc=1, device_id=partner, device_id_type=MESH)
    for step in range(NW):
        for dy in range(NY):
            if step or dy:
                pl.semaphore_signal(barrier, inc=1, device_id=(wide_at(step, 1), blks[dy]), device_id_type=MESH)

    for load in loads[:4]:
        load.wait()
    row = lax.broadcasted_iota(jnp.int32, (ROWS, ROWS), 0)
    col = lax.broadcasted_iota(jnp.int32, (ROWS, ROWS), 1)
    same = row % NI == col // NW

    def spread(value):
        return jnp.broadcast_to(jnp.concatenate([value] * NI, axis=1), (ROWS, ROWS))

    def one_hot(value):
        return jnp.where((spread(value) == row // NI) & same, 1.0, 0.0).astype(jnp.bfloat16)

    order = one_hot(owner[...])
    width = amps.shape[2]
    for j in range(4):
        lanes = slice(j * width // 4, (j + 1) * width // 4)
        piece = amps[:, :, lanes].reshape(ROWS, width // 4)
        value = jnp.dot(order, piece, preferred_element_type=jnp.float32).astype(jnp.bfloat16)
        stage[:, :, lanes] = value.reshape(NW, NI, width // 4)

    pl.semaphore_wait(barrier, NW * NY)

    mine = pltpu.make_async_copy(stage.at[w], got.at[0, 0], arrive.at[0])
    mine.start()
    for step in range(1, NW):
        to = wide_at(step, 1)
        remote(stage.at[to], got.at[0, step], sent.at[0], arrive.at[step], (to, b)).start()

    exchange = remote(ints, held.at[c], swap.at[0], swap.at[1], partner)
    exchange.start()

    up, down = (w, blks[1]), (w, blks[NY - 1])
    pairs = held.shape[2]

    def lay(part, group):
        piece = got[part, group * GROUP:(group + 1) * GROUP].reshape(GROUP * NI, width)
        place = (group // 4 * NY + PLACE[part]) * 64 + group % 4 * 16
        rows[place:place + 16, :] = piece

    def forward(group):
        for step in range(group * GROUP, (group + 1) * GROUP):
            chunk = got.at[0, step]
            await_bytes(chunk, arrive.at[step])
            remote(chunk, got.at[3, step], sent.at[1], from_down.at[step], up).start()
            remote(chunk, got.at[1, step], sent.at[2], from_up.at[step], down).start()
        lay(0, group)

    def relay(group):
        for step in range(group * GROUP, (group + 1) * GROUP):
            low, high = got.at[3, step], got.at[1, step]
            await_bytes(low, from_down.at[step])
            await_bytes(high, from_up.at[step])
            if step % 2 == 0:
                remote(low, got.at[2, step], sent.at[3], far.at[step], up).start()
            else:
                remote(high, got.at[2, step], sent.at[4], far.at[step], down).start()
        lay(3, group)
        lay(1, group)

    def finish(group):
        for step in range(group * GROUP, (group + 1) * GROUP):
            await_bytes(got.at[2, step], far.at[step])
        lay(2, group)

    def turn(core, k):
        lanes = pl.ds(pl.multiple_of((core * 2 + k) * pairs, pairs), pairs)
        turned[:, lanes] = held[core, k].T

    def contract(first, count):
        for n in range(4):
            lanes = slice(n * pairs, (n + 1) * pairs)
            value = jnp.dot(rows[first * 64:(first + count) * 64, :], turned[:, lanes],
                            preferred_element_type=jnp.float32)
            made[first * HALF:(first + count) * HALF, :, lanes] = value.astype(jnp.bfloat16).reshape(count * HALF, NI, pairs)

    def give(part, half):
        base = (half * NY + PLACE[part]) * HALF
        for n in range(HALF):
            step = half * HALF + n
            if part == 0 and step == 0:
                pltpu.make_async_copy(made.at[base], back.at[y, w], home.at[0]).start()
            else:
                remote(made.at[base + n], back.at[y, w], sent.at[5], home.at[part],
                       (wide_at(step, -1), blks[part])).start()

    loads[4].wait()
    turn(c, 0)
    forward(0)
    turn(c, 1)
    forward(1)
    forward(2)
    relay(0)

    pick = []
    for k in range(2):
        live = jnp.where(counts[...] > k, targets[k:k + 1, :], -1)
        chosen = lax.dot_general(one_hot(live), order, NT_DIMS, preferred_element_type=jnp.float32)
        pick.append(chosen.astype(jnp.bfloat16))

    exchange.wait_recv()
    turn(1 - c, 0)
    forward(3)
    relay(1)
    turn(1 - c, 1)
    contract(0, 1)
    give(0, 0)
    forward(4)
    relay(2)
    finish(0)
    forward(5)
    relay(3)
    finish(1)
    contract(1, 2)
    give(3, 0)
    give(1, 0)
    forward(6)
    relay(4)
    finish(2)
    forward(7)
    relay(5)
    finish(3)
    contract(3, 2)
    give(2, 0)
    give(0, 1)
    relay(6)
    relay(7)
    contract(5, 2)
    give(3, 1)
    give(1, 1)
    for group in range(4, GROUPS):
        finish(group)
    contract(7, 1)
    give(2, 1)

    for part in (0, 3, 1, 2):
        origin = lax.rem(y + NY - part, NY)
        await_bytes(back.at[origin], home.at[part])
        piece = back[origin].reshape(ROWS, 4 * pairs)
        for cc in range(2):
            total = jnp.dot(pick[0], piece[:, 2 * cc * pairs:(2 * cc + 1) * pairs], preferred_element_type=jnp.float32)
            total += jnp.dot(pick[1], piece[:, (2 * cc + 1) * pairs:(2 * cc + 2) * pairs], preferred_element_type=jnp.float32)
            lanes = pl.ds(pl.multiple_of((origin * 2 + cc) * pairs, pairs), pairs)
            out[:, :, lanes] = total.astype(jnp.bfloat16).reshape(NW, NI, pairs)

    await_bytes(stage.at[pl.ds(0, NW - 1)], sent.at[0])
    await_bytes(got.at[0], sent.at[1])
    await_bytes(got.at[0], sent.at[2])
    await_bytes(got.at[2, pl.ds(0, HALF)], sent.at[3])
    await_bytes(got.at[2, pl.ds(0, HALF)], sent.at[4])
    await_bytes(made.at[pl.ds(0, 8 * HALF - 1)], sent.at[5])
    exchange.wait_send()


def body(amplitudes, integrals, owner, targets, counts):
    amps, ints = amplitudes[:, 0], integrals[0]
    width = amps.shape[2]
    pairs = ints.shape[1]
    dma = pltpu.SemaphoreType.DMA
    out = pl.pallas_call(
        kernel,
        out_shape=jax.ShapeDtypeStruct((NW, NI, 2 * NY * pairs), jnp.bfloat16),
        in_specs=[pl.BlockSpec(memory_space=pltpu.HBM)] * 5,
        out_specs=pl.BlockSpec(memory_space=pltpu.VMEM),
        scratch_shapes=[
            pltpu.VMEM((1, NW), jnp.int32),
            pltpu.VMEM((2, NW), jnp.int32),
            pltpu.VMEM((1, NW), jnp.int32),
            pltpu.VMEM((NI, NW, width), jnp.bfloat16),
            pltpu.VMEM((NW, NI, width), jnp.bfloat16),
            pltpu.VMEM((NY, NW, NI, width), jnp.bfloat16),
            pltpu.VMEM((NY * ROWS, width), jnp.bfloat16),
            pltpu.VMEM((2, 2, pairs, width), jnp.bfloat16),
            pltpu.VMEM((width, 4 * pairs), jnp.bfloat16),
            pltpu.VMEM((NY * NW, NI, 4 * pairs), jnp.bfloat16),
            pltpu.VMEM((NY, NW, NI, 4 * pairs), jnp.bfloat16),
            dma((NW,)), dma((NW,)), dma((NW,)), dma((NW,)), dma((NY,)), dma((5,)), dma((6,)), dma((2,)),
        ],
        compiler_params=pltpu.CompilerParams(
            collective_id=0, has_side_effects=True, vmem_limit_bytes=48 << 20),
        name="ladder",
    )(*(pltpu.with_memory_space_constraint(a, pltpu.HBM) for a in (owner[None], targets.T, counts[None], amps, ints)))
    return out[:, :, None, :]


def solution(mesh):
    placed = (P("blk", "wide", None, None), P("wide", None, "blk", None), P(), P(), P())
    return jax.shard_map(
        body, mesh=mesh, in_specs=placed, out_specs=P(None, "blk", "wide", None), check_vma=False
    )
```

```python
import functools
import jax
import jax.numpy as jnp
from jax import lax
from jax.experimental import pallas as pl
from jax.experimental.pallas import tpu as pltpu
from jax.sharding import PartitionSpec as P

MESH = pl.DeviceIdType.MESH
NX, NY, NZ = 4, 4, 8
NW = NX * NZ
NI = 4
ROWS = NW * NI
GROUP = 4
GROUPS = NW // GROUP
HALF = NW // 2
DZ = (0, 1, 7, 4, 3, 5, 2, 6)
PLACE = (0, 2, 3, 1)
NT_DIMS = (((1,), (1,)), ((), ()))


def kernel(owner_hbm, targets_hbm, counts_hbm, amps_hbm, ints, out,
           owner, targets, counts, amps, stage, got, rows, held, turned, made, back, summed, final,
           arrive, from_up, from_down, far, home, last, local, sent, swap):
    w, b = lax.axis_index("wide"), lax.axis_index("blk")
    y, c = b // 2, b % 2
    xs = [lax.rem(w // NZ + d, NX) * NZ for d in range(NX)]
    zs = [lax.rem(w % NZ + d, NZ) for d in range(NZ)]
    blks = [lax.rem(y + d, NY) * 2 + c for d in range(NY)]

    def wide_at(step, sign):
        dz, dx = DZ[step // NX], step % NX
        return xs[sign * dx % NX] + zs[sign * dz % NZ]

    def remote(src, dst, send, recv, device):
        return pltpu.make_async_remote_copy(
            src_ref=src, dst_ref=dst, send_sem=send, recv_sem=recv,
            device_id=device, device_id_type=MESH)

    def await_bytes(ref, sem):
        pltpu.make_async_copy(ref, ref, sem).wait()

    partner = (w, y * 2 + 1 - c)

    loads = [pltpu.make_async_copy(src, dst, local.at[n]) for n, (src, dst) in enumerate((
        (amps_hbm, amps), (owner_hbm, owner), (targets_hbm, targets), (counts_hbm, counts), (ints, held.at[c])))]
    for load in loads:
        load.start()

    barrier = pltpu.get_barrier_semaphore()
    pl.semaphore_signal(barrier, inc=1, device_id=partner, device_id_type=MESH)
    for dy in range(1, NY):
        pl.semaphore_signal(barrier, inc=1, device_id=(w, blks[dy]), device_id_type=MESH)
    for step in range(1, NW):
        pl.semaphore_signal(barrier, inc=1, device_id=(wide_at(step, 1), b), device_id_type=MESH)

    for load in loads[:4]:
        load.wait()
    row = lax.broadcasted_iota(jnp.int32, (ROWS, ROWS), 0)
    col = lax.broadcasted_iota(jnp.int32, (ROWS, ROWS), 1)
    same = row % NI == col // NW

    def spread(value):
        return jnp.broadcast_to(jnp.concatenate([value] * NI, axis=1), (ROWS, ROWS))

    def one_hot(value):
        return jnp.where((spread(value) == row // NI) & same, 1.0, 0.0).astype(jnp.bfloat16)

    order = one_hot(owner[...])
    width = amps.shape[2]
    for j in range(4):
        lanes = slice(j * width // 4, (j + 1) * width // 4)
        piece = amps[:, :, lanes].reshape(ROWS, width // 4)
        value = jnp.dot(order, piece, preferred_element_type=jnp.float32).astype(jnp.bfloat16)
        stage[:, :, lanes] = value.reshape(NW, NI, width // 4)

    pl.semaphore_wait(barrier, NW + NY - 1)

    mine = pltpu.make_async_copy(stage.at[w], got.at[0, 0], arrive.at[0])
    mine.start()
    for step in range(1, NW):
        to = wide_at(step, 1)
        remote(stage.at[to], got.at[0, step], sent.at[0], arrive.at[step], (to, b)).start()

    exchange = remote(ints, held.at[c], swap.at[0], swap.at[1], partner)
    exchange.start()

    up, down = (w, blks[1]), (w, blks[NY - 1])
    pairs = held.shape[2]

    def lay(part, group):
        piece = got[part, group * GROUP:(group + 1) * GROUP].reshape(GROUP * NI, width)
        place = (group // 4 * NY + PLACE[part]) * 64 + group % 4 * 16
        rows[place:place + 16, :] = piece

    def forward(group):
        for step in range(group * GROUP, (group + 1) * GROUP):
            chunk = got.at[0, step]
            await_bytes(chunk, arrive.at[step])
            remote(chunk, got.at[3, step], sent.at[1], from_down.at[step], up).start()
            remote(chunk, got.at[1, step], sent.at[2], from_up.at[step], down).start()
        lay(0, group)

    def relay(group):
        for step in range(group * GROUP, (group + 1) * GROUP):
            low, high = got.at[3, step], got.at[1, step]
            await_bytes(low, from_down.at[step])
            await_bytes(high, from_up.at[step])
            if step % 2 == 0:
                remote(low, got.at[2, step], sent.at[3], far.at[step], up).start()
            else:
                remote(high, got.at[2, step], sent.at[4], far.at[step], down).start()
        lay(3, group)
        lay(1, group)

    def finish(group):
        for step in range(group * GROUP, (group + 1) * GROUP):
            await_bytes(got.at[2, step], far.at[step])
        lay(2, group)

    def turn(core, k):
        lanes = pl.ds(pl.multiple_of((core * 2 + k) * pairs, pairs), pairs)
        turned[:, lanes] = held[core, k].T

    def contract(first, count, spare=0):
        for n in range(4):
            lanes = slice(n * pairs, (n + 1) * pairs)
            value = jnp.dot(rows[(first - spare) * 64:(first + count) * 64, :], turned[:, lanes],
                            preferred_element_type=jnp.float32)[spare * 64:]
            made[first * HALF:(first + count) * HALF, :, lanes] = value.astype(jnp.bfloat16).reshape(count * HALF, NI, pairs)

    def give(part, half):
        base = (half * NY + PLACE[part]) * HALF
        for n in range(HALF):
            step = half * HALF + n
            if step == 0:
                pltpu.make_async_copy(made.at[base], back.at[part, w], home.at[part]).start()
            else:
                remote(made.at[base + n], back.at[part, w], sent.at[5], home.at[part],
                       (wide_at(step, -1), b)).start()

    def sumup(part):
        await_bytes(back.at[part], home.at[part])
        piece = back[part].reshape(ROWS, 4 * pairs)
        for cc in range(2):
            total = jnp.dot(pick[0], piece[:, 2 * cc * pairs:(2 * cc + 1) * pairs], preferred_element_type=jnp.float32)
            total += jnp.dot(pick[1], piece[:, (2 * cc + 1) * pairs:(2 * cc + 2) * pairs], preferred_element_type=jnp.float32)
            total = total.astype(jnp.bfloat16).reshape(NW, NI, pairs)
            if part == 0:
                out[:, :, pl.ds(pl.multiple_of((y * 2 + cc) * pairs, pairs), pairs)] = total
            else:
                summed[part, :, :, cc * pairs:(cc + 1) * pairs] = total
        if part:
            remote(summed.at[part], final.at[part], sent.at[6], last.at[part], (w, blks[part])).start()

    def settle(part):
        await_bytes(final.at[part], last.at[part])
        origin = lax.rem(y + NY - part, NY)
        out[:, :, pl.ds(pl.multiple_of(origin * 2 * pairs, 2 * pairs), 2 * pairs)] = final[part]

    loads[4].wait()
    turn(c, 0)
    forward(0)
    turn(c, 1)
    forward(1)
    forward(2)
    relay(0)

    pick = []
    for k in range(2):
        live = jnp.where(counts[...] > k, targets[k:k + 1, :], -1)
        chosen = lax.dot_general(one_hot(live), order, NT_DIMS, preferred_element_type=jnp.float32)
        pick.append(chosen.astype(jnp.bfloat16))

    exchange.wait_recv()
    turn(1 - c, 0)
    forward(3)
    relay(1)
    turn(1 - c, 1)
    contract(0, 1)
    give(0, 0)
    forward(4)
    relay(2)
    finish(0)
    forward(5)
    relay(3)
    finish(1)
    contract(1, 2)
    give(3, 0)
    give(1, 0)
    forward(6)
    relay(4)
    finish(2)
    forward(7)
    relay(5)
    finish(3)
    contract(3, 2)
    give(2, 0)
    give(0, 1)
    relay(6)
    relay(7)
    contract(5, 2)
    give(3, 1)
    give(1, 1)
    for group in range(4, GROUPS):
        finish(group)
    contract(7, 1, 1)
    give(2, 1)

    sumup(0)
    sumup(3)
    sumup(1)
    sumup(2)
    settle(3)
    settle(1)
    settle(2)

    await_bytes(stage.at[pl.ds(0, NW - 1)], sent.at[0])
    await_bytes(got.at[0], sent.at[1])
    await_bytes(got.at[0], sent.at[2])
    await_bytes(got.at[2, pl.ds(0, HALF)], sent.at[3])
    await_bytes(got.at[2, pl.ds(0, HALF)], sent.at[4])
    await_bytes(made.at[pl.ds(0, NY * (NW - 1))], sent.at[5])
    await_bytes(summed.at[pl.ds(0, NY - 1)], sent.at[6])
    exchange.wait_send()


def body(amplitudes, integrals, owner, targets, counts):
    amps, ints = amplitudes[:, 0], integrals[0]
    width = amps.shape[2]
    pairs = ints.shape[1]
    dma = pltpu.SemaphoreType.DMA
    out = pl.pallas_call(
        kernel,
        out_shape=jax.ShapeDtypeStruct((NW, NI, 2 * NY * pairs), jnp.bfloat16),
        in_specs=[pl.BlockSpec(memory_space=pltpu.HBM)] * 5,
        out_specs=pl.BlockSpec(memory_space=pltpu.VMEM),
        scratch_shapes=[
            pltpu.VMEM((1, NW), jnp.int32),
            pltpu.VMEM((2, NW), jnp.int32),
            pltpu.VMEM((1, NW), jnp.int32),
            pltpu.VMEM((NI, NW, width), jnp.bfloat16),
            pltpu.VMEM((NW, NI, width), jnp.bfloat16),
            pltpu.VMEM((NY, NW, NI, width), jnp.bfloat16),
            pltpu.VMEM((NY * ROWS, width), jnp.bfloat16),
            pltpu.VMEM((2, 2, pairs, width), jnp.bfloat16),
            pltpu.VMEM((width, 4 * pairs), jnp.bfloat16),
            pltpu.VMEM((NY * NW, NI, 4 * pairs), jnp.bfloat16),
            pltpu.VMEM((NY, NW, NI, 4 * pairs), jnp.bfloat16),
            pltpu.VMEM((NY, NW, NI, 2 * pairs), jnp.bfloat16),
            pltpu.VMEM((NY, NW, NI, 2 * pairs), jnp.bfloat16),
            dma((NW,)), dma((NW,)), dma((NW,)), dma((NW,)), dma((NY,)), dma((NY,)), dma((5,)), dma((7,)), dma((2,)),
        ],
        compiler_params=pltpu.CompilerParams(
            collective_id=0, has_side_effects=True, vmem_limit_bytes=48 << 20),
        name="ladder",
    )(*(pltpu.with_memory_space_constraint(a, pltpu.HBM) for a in (owner[None], targets.T, counts[None], amps, ints)))
    return out[:, :, None, :]


def solution(mesh):
    placed = (P("blk", "wide", None, None), P("wide", None, "blk", None), P(), P(), P())
    return jax.shard_map(
        body, mesh=mesh, in_specs=placed, out_specs=P(None, "blk", "wide", None), check_vma=False
    )
```

```python
import functools
import jax
import jax.numpy as jnp
from jax import lax
from jax.experimental import pallas as pl
from jax.experimental.pallas import tpu as pltpu
from jax.sharding import PartitionSpec as P

MESH = pl.DeviceIdType.MESH
NX, NY, NZ = 4, 4, 8
NW = NX * NZ
NI = 4
ROWS = NW * NI
GROUP = 4
GROUPS = NW // GROUP
DZ = (0, 1, 7, 4, 3, 5, 2, 6)
BLOCKS = ((0, 0, 4), (3, 0, 4), (1, 0, 4), (0, 4, 6), (0, 6, 8), (3, 4, 6), (1, 4, 6), (2, 0, 4),
          (3, 6, 8), (1, 6, 8), (2, 4, 6), (2, 6, 8))
SLOT = {}
for _part, _first, _end in BLOCKS:
    for _group in range(_first, _end):
        SLOT[_part, _group] = len(SLOT)
NT_DIMS = (((1,), (1,)), ((), ()))


def kernel(owner_hbm, targets_hbm, counts_hbm, amps_hbm, ints, out,
           owner, targets, counts, amps, stage, got, rows, held, turned, made, back, summed, final,
           arrive, from_up, from_down, far, home, last, local, sent, swap):
    w, b = lax.axis_index("wide"), lax.axis_index("blk")
    y, c = b // 2, b % 2
    xs = [lax.rem(w // NZ + d, NX) * NZ for d in range(NX)]
    zs = [lax.rem(w % NZ + d, NZ) for d in range(NZ)]
    blks = [lax.rem(y + d, NY) * 2 + c for d in range(NY)]

    def wide_at(step, sign):
        dz, dx = DZ[step // NX], step % NX
        return xs[sign * dx % NX] + zs[sign * dz % NZ]

    def remote(src, dst, send, recv, device):
        return pltpu.make_async_remote_copy(
            src_ref=src, dst_ref=dst, send_sem=send, recv_sem=recv,
            device_id=device, device_id_type=MESH)

    def await_bytes(ref, sem):
        pltpu.make_async_copy(ref, ref, sem).wait()

    partner = (w, y * 2 + 1 - c)

    loads = [pltpu.make_async_copy(src, dst, local.at[n]) for n, (src, dst) in enumerate((
        (amps_hbm, amps), (owner_hbm, owner), (targets_hbm, targets), (counts_hbm, counts), (ints, held.at[c])))]
    for load in loads:
        load.start()

    barrier = pltpu.get_barrier_semaphore()
    pl.semaphore_signal(barrier, inc=1, device_id=partner, device_id_type=MESH)
    for dy in (1, 3):
        pl.semaphore_signal(barrier, inc=1, device_id=(w, blks[dy]), device_id_type=MESH)
    for step in range(NW):
        for dy in (0, 2):
            if step or dy:
                pl.semaphore_signal(barrier, inc=1, device_id=(wide_at(step, 1), blks[dy]), device_id_type=MESH)

    for load in loads[:4]:
        load.wait()
    row = lax.broadcasted_iota(jnp.int32, (ROWS, ROWS), 0)
    col = lax.broadcasted_iota(jnp.int32, (ROWS, ROWS), 1)
    same = row % NI == col // NW

    def spread(value):
        return jnp.broadcast_to(jnp.concatenate([value] * NI, axis=1), (ROWS, ROWS))

    def one_hot(value):
        return jnp.where((spread(value) == row // NI) & same, 1.0, 0.0).astype(jnp.bfloat16)

    order = one_hot(owner[...])
    width = amps.shape[2]
    for j in range(4):
        lanes = slice(j * width // 4, (j + 1) * width // 4)
        piece = amps[:, :, lanes].reshape(ROWS, width // 4)
        value = jnp.dot(order, piece, preferred_element_type=jnp.float32).astype(jnp.bfloat16)
        stage[:, :, lanes] = value.reshape(NW, NI, width // 4)

    pl.semaphore_wait(barrier, 2 * NW + 2)

    mine = pltpu.make_async_copy(stage.at[w], got.at[0, 0], arrive.at[0])
    mine.start()
    for step in range(1, NW):
        to = wide_at(step, 1)
        remote(stage.at[to], got.at[0, step], sent.at[0], arrive.at[step], (to, b)).start()

    exchange = remote(ints, held.at[c], swap.at[0], swap.at[1], partner)
    exchange.start()

    up, down = (w, blks[1]), (w, blks[NY - 1])
    pairs = held.shape[2]

    def lay(part, group):
        piece = got[part, group * GROUP:(group + 1) * GROUP].reshape(GROUP * NI, width)
        place = SLOT[part, group] * GROUP * NI
        rows[place:place + GROUP * NI, :] = piece

    def forward(group):
        for step in range(group * GROUP, (group + 1) * GROUP):
            chunk = got.at[0, step]
            await_bytes(chunk, arrive.at[step])
            remote(chunk, got.at[3, step], sent.at[1], from_down.at[step], up).start()
            remote(chunk, got.at[1, step], sent.at[2], from_up.at[step], down).start()
        lay(0, group)

    def relay(group):
        for step in range(group * GROUP, (group + 1) * GROUP):
            low, high = got.at[3, step], got.at[1, step]
            await_bytes(low, from_down.at[step])
            await_bytes(high, from_up.at[step])
            if step % 2 == 0:
                remote(low, got.at[2, step], sent.at[3], far.at[step], up).start()
            else:
                remote(high, got.at[2, step], sent.at[4], far.at[step], down).start()
        lay(3, group)
        lay(1, group)

    def finish(group):
        for step in range(group * GROUP, (group + 1) * GROUP):
            await_bytes(got.at[2, step], far.at[step])
        lay(2, group)

    def turn(core, k):
        lanes = pl.ds(pl.multiple_of((core * 2 + k) * pairs, pairs), pairs)
        turned[:, lanes] = held[core, k].T

    def contract(first, end, spare=0):
        for n in range(4):
            lanes = slice(n * pairs, (n + 1) * pairs)
            value = jnp.dot(rows[first - spare:end, :], turned[:, lanes], preferred_element_type=jnp.float32)[spare:]
            made[first // NI:end // NI, :, lanes] = value.astype(jnp.bfloat16).reshape((end - first) // NI, NI, pairs)

    def give(part, first, end):
        for step in range(first * GROUP, end * GROUP):
            chunk = made.at[SLOT[part, step // GROUP] * GROUP + step % GROUP]
            if part == 2:
                remote(chunk, back.at[part, w], sent.at[5], home.at[part], (wide_at(step, -1), blks[2])).start()
            elif step == 0:
                pltpu.make_async_copy(chunk, back.at[part, w], home.at[part]).start()
            else:
                remote(chunk, back.at[part, w], sent.at[5], home.at[part], (wide_at(step, -1), b)).start()

    def sumup(part):
        await_bytes(back.at[part], home.at[part])
        piece = back[part].reshape(ROWS, 4 * pairs)
        for cc in range(2):
            total = jnp.dot(pick[0], piece[:, 2 * cc * pairs:(2 * cc + 1) * pairs], preferred_element_type=jnp.float32)
            total += jnp.dot(pick[1], piece[:, (2 * cc + 1) * pairs:(2 * cc + 2) * pairs], preferred_element_type=jnp.float32)
            total = total.astype(jnp.bfloat16).reshape(NW, NI, pairs)
            if part % 2 == 0:
                origin = lax.rem(y + part, NY)
                out[:, :, pl.ds(pl.multiple_of((origin * 2 + cc) * pairs, pairs), pairs)] = total
            else:
                summed[part, :, :, cc * pairs:(cc + 1) * pairs] = total
        if part % 2:
            remote(summed.at[part], final.at[part], sent.at[6], last.at[part], (w, blks[part])).start()

    def settle(part):
        await_bytes(final.at[part], last.at[part])
        origin = lax.rem(y + NY - part, NY)
        out[:, :, pl.ds(pl.multiple_of(origin * 2 * pairs, 2 * pairs), 2 * pairs)] = final[part]

    loads[4].wait()
    turn(c, 0)
    forward(0)
    turn(c, 1)
    forward(1)
    forward(2)
    relay(0)

    pick = []
    for k in range(2):
        live = jnp.where(counts[...] > k, targets[k:k + 1, :], -1)
        chosen = lax.dot_general(one_hot(live), order, NT_DIMS, preferred_element_type=jnp.float32)
        pick.append(chosen.astype(jnp.bfloat16))

    exchange.wait_recv()
    turn(1 - c, 0)
    forward(3)
    relay(1)
    turn(1 - c, 1)
    contract(0, 64)
    give(0, 0, 4)
    forward(4)
    relay(2)
    finish(0)
    forward(5)
    relay(3)
    finish(1)
    contract(64, 224)
    give(3, 0, 4)
    give(1, 0, 4)
    give(0, 4, 6)
    forward(6)
    relay(4)
    finish(2)
    forward(7)
    relay(5)
    finish(3)
    contract(224, 384)
    give(3, 4, 6)
    give(1, 4, 6)
    give(0, 6, 8)
    relay(6)
    relay(7)
    give(2, 0, 4)
    finish(4)
    finish(5)
    contract(384, 480, 32)
    give(3, 6, 8)
    give(1, 6, 8)
    give(2, 4, 6)
    finish(6)
    finish(7)
    contract(480, 512, 96)
    give(2, 6, 8)

    sumup(3)
    sumup(1)
    sumup(0)
    sumup(2)
    settle(3)
    settle(1)

    await_bytes(stage.at[pl.ds(0, NW - 1)], sent.at[0])
    await_bytes(got.at[0], sent.at[1])
    await_bytes(got.at[0], sent.at[2])
    await_bytes(got.at[2, pl.ds(0, NW // 2)], sent.at[3])
    await_bytes(got.at[2, pl.ds(0, NW // 2)], sent.at[4])
    await_bytes(made.at[pl.ds(0, NY * NW - 3)], sent.at[5])
    await_bytes(summed.at[pl.ds(0, 2)], sent.at[6])
    exchange.wait_send()


def body(amplitudes, integrals, owner, targets, counts):
    amps, ints = amplitudes[:, 0], integrals[0]
    width = amps.shape[2]
    pairs = ints.shape[1]
    dma = pltpu.SemaphoreType.DMA
    out = pl.pallas_call(
        kernel,
        out_shape=jax.ShapeDtypeStruct((NW, NI, 2 * NY * pairs), jnp.bfloat16),
        in_specs=[pl.BlockSpec(memory_space=pltpu.HBM)] * 5,
        out_specs=pl.BlockSpec(memory_space=pltpu.VMEM),
        scratch_shapes=[
            pltpu.VMEM((1, NW), jnp.int32),
            pltpu.VMEM((2, NW), jnp.int32),
            pltpu.VMEM((1, NW), jnp.int32),
            pltpu.VMEM((NI, NW, width), jnp.bfloat16),
            pltpu.VMEM((NW, NI, width), jnp.bfloat16),
            pltpu.VMEM((NY, NW, NI, width), jnp.bfloat16),
            pltpu.VMEM((NY * ROWS, width), jnp.bfloat16),
            pltpu.VMEM((2, 2, pairs, width), jnp.bfloat16),
            pltpu.VMEM((width, 4 * pairs), jnp.bfloat16),
            pltpu.VMEM((NY * NW, NI, 4 * pairs), jnp.bfloat16),
            pltpu.VMEM((NY, NW, NI, 4 * pairs), jnp.bfloat16),
            pltpu.VMEM((NY, NW, NI, 2 * pairs), jnp.bfloat16),
            pltpu.VMEM((NY, NW, NI, 2 * pairs), jnp.bfloat16),
            dma((NW,)), dma((NW,)), dma((NW,)), dma((NW,)), dma((NY,)), dma((NY,)), dma((5,)), dma((7,)), dma((2,)),
        ],
        compiler_params=pltpu.CompilerParams(
            collective_id=0, has_side_effects=True, vmem_limit_bytes=48 << 20),
        name="ladder",
    )(*(pltpu.with_memory_space_constraint(a, pltpu.HBM) for a in (owner[None], targets.T, counts[None], amps, ints)))
    return out[:, :, None, :]


def solution(mesh):
    placed = (P("blk", "wide", None, None), P("wide", None, "blk", None), P(), P(), P())
    return jax.shard_map(
        body, mesh=mesh, in_specs=placed, out_specs=P(None, "blk", "wide", None), check_vma=False
    )
```

```python
import functools
import jax
import jax.numpy as jnp
from jax import lax
from jax.experimental import pallas as pl
from jax.experimental.pallas import tpu as pltpu
from jax.sharding import PartitionSpec as P

MESH = pl.DeviceIdType.MESH
NX, NY, NZ = 4, 4, 8
NW = NX * NZ
NI = 4
ROWS = NW * NI
GROUP = 4
PIECES = 4
GROUPS = NW // GROUP
ORDER = ((0, 0), (1, 0), (3, 0), (0, 1), (0, 7), (2, 0), (1, 1), (3, 1), (1, 7), (3, 7), (2, 1), (2, 7)) + tuple(
    (dx, dz) for dz in (4, 3, 5, 2, 6) for dx in range(4))
BLOCKS = ((0, 0, 4), (3, 0, 4), (1, 0, 4), (0, 4, 6), (0, 6, 8), (3, 4, 6), (1, 4, 6), (2, 0, 4),
          (3, 6, 8), (1, 6, 8), (2, 4, 6), (2, 6, 8))
SLOT = {}
for _part, _first, _end in BLOCKS:
    for _group in range(_first, _end):
        SLOT[_part, _group] = len(SLOT)
NT_DIMS = (((1,), (1,)), ((), ()))


def kernel(owner_hbm, targets_hbm, counts_hbm, amps_hbm, ints, out,
           owner, targets, counts, amps, stage, got, rows, held, turned, made, back, summed, final,
           arrive, from_up, from_down, far, home, last, local, sent, swap):
    w, b = lax.axis_index("wide"), lax.axis_index("blk")
    y, c = b // 2, b % 2
    xs = [lax.rem(w // NZ + d, NX) * NZ for d in range(NX)]
    zs = [lax.rem(w % NZ + d, NZ) for d in range(NZ)]
    blks = [lax.rem(y + d, NY) * 2 + c for d in range(NY)]

    def wide_at(step, sign):
        dx, dz = ORDER[step]
        return xs[sign * dx % NX] + zs[sign * dz % NZ]

    def remote(src, dst, send, recv, device):
        return pltpu.make_async_remote_copy(
            src_ref=src, dst_ref=dst, send_sem=send, recv_sem=recv,
            device_id=device, device_id_type=MESH)

    def await_bytes(ref, sem):
        pltpu.make_async_copy(ref, ref, sem).wait()

    partner = (w, y * 2 + 1 - c)

    loads = [pltpu.make_async_copy(src, dst, local.at[n]) for n, (src, dst) in enumerate((
        (amps_hbm, amps), (owner_hbm, owner), (targets_hbm, targets), (counts_hbm, counts), (ints, held.at[c])))]
    for load in loads:
        load.start()

    barrier = pltpu.get_barrier_semaphore()
    pl.semaphore_signal(barrier, inc=1, device_id=partner, device_id_type=MESH)
    for dy in (1, 3):
        pl.semaphore_signal(barrier, inc=1, device_id=(w, blks[dy]), device_id_type=MESH)
    for step in range(NW):
        for dy in (0, 2):
            if step or dy:
                pl.semaphore_signal(barrier, inc=1, device_id=(wide_at(step, 1), blks[dy]), device_id_type=MESH)

    for load in loads[:4]:
        load.wait()
    row = lax.broadcasted_iota(jnp.int32, (ROWS, ROWS), 0)
    col = lax.broadcasted_iota(jnp.int32, (ROWS, ROWS), 1)
    same = row % NI == col // NW

    def spread(value):
        return jnp.broadcast_to(jnp.concatenate([value] * NI, axis=1), (ROWS, ROWS))

    def one_hot(value):
        return jnp.where((spread(value) == row // NI) & same, 1.0, 0.0).astype(jnp.bfloat16)

    order = one_hot(owner[...])
    width = amps.shape[2]
    for j in range(4):
        lanes = slice(j * width // 4, (j + 1) * width // 4)
        piece = amps[:, :, lanes].reshape(ROWS, width // 4)
        value = jnp.dot(order, piece, preferred_element_type=jnp.float32).astype(jnp.bfloat16)
        stage[:, :, lanes] = value.reshape(NW, NI, width // 4)

    pl.semaphore_wait(barrier, 2 * NW + 2)

    mine = pltpu.make_async_copy(stage.at[w], got.at[0, 0], arrive.at[0])
    mine.start()
    for step in range(1, NW):
        to = wide_at(step, 1)
        for n in range(PIECES):
            lanes = pl.ds(n * (width // PIECES), width // PIECES)
            remote(stage.at[to, :, lanes], got.at[0, step, :, lanes], sent.at[0], arrive.at[step], (to, b)).start()

    exchange = remote(ints, held.at[c], swap.at[0], swap.at[1], partner)
    exchange.start()

    up, down = (w, blks[1]), (w, blks[NY - 1])
    pairs = held.shape[2]

    def lay(part, group):
        piece = got[part, group * GROUP:(group + 1) * GROUP].reshape(GROUP * NI, width)
        place = SLOT[part, group] * GROUP * NI
        rows[place:place + GROUP * NI, :] = piece

    def forward(group):
        for step in range(group * GROUP, (group + 1) * GROUP):
            chunk = got.at[0, step]
            await_bytes(chunk, arrive.at[step])
            remote(chunk, got.at[3, step], sent.at[1], from_down.at[step], up).start()
            remote(chunk, got.at[1, step], sent.at[2], from_up.at[step], down).start()
        lay(0, group)

    def relay(group):
        for step in range(group * GROUP, (group + 1) * GROUP):
            low, high = got.at[3, step], got.at[1, step]
            await_bytes(low, from_down.at[step])
            await_bytes(high, from_up.at[step])
            if step % 2 == 0:
                remote(low, got.at[2, step], sent.at[3], far.at[step], up).start()
            else:
                remote(high, got.at[2, step], sent.at[4], far.at[step], down).start()
        lay(3, group)
        lay(1, group)

    def finish(group):
        for step in range(group * GROUP, (group + 1) * GROUP):
            await_bytes(got.at[2, step], far.at[step])
        lay(2, group)

    def turn(core, k):
        lanes = pl.ds(pl.multiple_of((core * 2 + k) * pairs, pairs), pairs)
        turned[:, lanes] = held[core, k].T

    def contract(first, end, spare=0, lanes=(0, 1, 2, 3)):
        for n in lanes:
            cols = slice(n * pairs, (n + 1) * pairs)
            value = jnp.dot(rows[first - spare:end, :], turned[:, cols], preferred_element_type=jnp.float32)[spare:]
            made[first // NI:end // NI, :, cols] = value.astype(jnp.bfloat16).reshape((end - first) // NI, NI, pairs)

    def give(part, first, end, lanes=slice(None)):
        for step in range(first * GROUP, end * GROUP):
            chunk = made.at[SLOT[part, step // GROUP] * GROUP + step % GROUP, :, lanes]
            there = back.at[part, w, :, lanes]
            if part == 2:
                remote(chunk, there, sent.at[5], home.at[part], (wide_at(step, -1), blks[2])).start()
            elif step == 0:
                pltpu.make_async_copy(chunk, there, home.at[part]).start()
            else:
                remote(chunk, there, sent.at[5], home.at[part], (wide_at(step, -1), b)).start()

    def sumup(part):
        await_bytes(back.at[part], home.at[part])
        piece = back[part].reshape(ROWS, 4 * pairs)
        for cc in range(2):
            total = jnp.dot(pick[0], piece[:, 2 * cc * pairs:(2 * cc + 1) * pairs], preferred_element_type=jnp.float32)
            total += jnp.dot(pick[1], piece[:, (2 * cc + 1) * pairs:(2 * cc + 2) * pairs], preferred_element_type=jnp.float32)
            total = total.astype(jnp.bfloat16).reshape(NW, NI, pairs)
            if part % 2 == 0:
                origin = lax.rem(y + part, NY)
                out[:, :, pl.ds(pl.multiple_of((origin * 2 + cc) * pairs, pairs), pairs)] = total
            else:
                summed[part, :, :, cc * pairs:(cc + 1) * pairs] = total
        if part % 2:
            remote(summed.at[part], final.at[part], sent.at[6], last.at[part], (w, blks[part])).start()

    def settle(part):
        await_bytes(final.at[part], last.at[part])
        origin = lax.rem(y + NY - part, NY)
        out[:, :, pl.ds(pl.multiple_of(origin * 2 * pairs, 2 * pairs), 2 * pairs)] = final[part]

    forward(0)
    loads[4].wait()
    turn(c, 0)
    forward(1)
    turn(c, 1)
    forward(2)
    relay(0)

    pick = []
    for k in range(2):
        live = jnp.where(counts[...] > k, targets[k:k + 1, :], -1)
        chosen = lax.dot_general(one_hot(live), order, NT_DIMS, preferred_element_type=jnp.float32)
        pick.append(chosen.astype(jnp.bfloat16))

    exchange.wait_recv()
    turn(1 - c, 0)
    forward(3)
    relay(1)
    turn(1 - c, 1)
    contract(0, 64)
    give(0, 0, 4)
    forward(4)
    relay(2)
    finish(0)
    forward(5)
    relay(3)
    finish(1)
    contract(64, 224)
    give(3, 0, 4)
    give(1, 0, 4)
    give(0, 4, 6)
    forward(6)
    relay(4)
    finish(2)
    forward(7)
    relay(5)
    finish(3)
    contract(224, 384)
    give(3, 4, 6)
    give(1, 4, 6)
    give(0, 6, 8)
    relay(6)
    relay(7)
    give(2, 0, 4)
    finish(4)
    finish(5)
    contract(384, 480, 32)
    give(3, 6, 8)
    give(1, 6, 8)
    give(2, 4, 6)
    finish(6)
    finish(7)
    for cc in range(2):
        contract(480, 512, 96, (2 * cc, 2 * cc + 1))
        give(2, 6, 8, pl.ds(2 * cc * pairs, 2 * pairs))

    sumup(3)
    sumup(1)
    sumup(0)
    sumup(2)
    settle(3)
    settle(1)

    await_bytes(stage.at[pl.ds(0, NW - 1)], sent.at[0])
    await_bytes(got.at[0], sent.at[1])
    await_bytes(got.at[0], sent.at[2])
    await_bytes(got.at[2, pl.ds(0, NW // 2)], sent.at[3])
    await_bytes(got.at[2, pl.ds(0, NW // 2)], sent.at[4])
    await_bytes(made.at[pl.ds(0, NY * NW - 3)], sent.at[5])
    await_bytes(summed.at[pl.ds(0, 2)], sent.at[6])
    exchange.wait_send()


def body(amplitudes, integrals, owner, targets, counts):
    amps, ints = amplitudes[:, 0], integrals[0]
    width = amps.shape[2]
    pairs = ints.shape[1]
    dma = pltpu.SemaphoreType.DMA
    out = pl.pallas_call(
        kernel,
        out_shape=jax.ShapeDtypeStruct((NW, NI, 2 * NY * pairs), jnp.bfloat16),
        in_specs=[pl.BlockSpec(memory_space=pltpu.HBM)] * 5,
        out_specs=pl.BlockSpec(memory_space=pltpu.VMEM),
        scratch_shapes=[
            pltpu.VMEM((1, NW), jnp.int32),
            pltpu.VMEM((2, NW), jnp.int32),
            pltpu.VMEM((1, NW), jnp.int32),
            pltpu.VMEM((NI, NW, width), jnp.bfloat16),
            pltpu.VMEM((NW, NI, width), jnp.bfloat16),
            pltpu.VMEM((NY, NW, NI, width), jnp.bfloat16),
            pltpu.VMEM((NY * ROWS, width), jnp.bfloat16),
            pltpu.VMEM((2, 2, pairs, width), jnp.bfloat16),
            pltpu.VMEM((width, 4 * pairs), jnp.bfloat16),
            pltpu.VMEM((NY * NW, NI, 4 * pairs), jnp.bfloat16),
            pltpu.VMEM((NY, NW, NI, 4 * pairs), jnp.bfloat16),
            pltpu.VMEM((NY, NW, NI, 2 * pairs), jnp.bfloat16),
            pltpu.VMEM((NY, NW, NI, 2 * pairs), jnp.bfloat16),
            dma((NW,)), dma((NW,)), dma((NW,)), dma((NW,)), dma((NY,)), dma((NY,)), dma((5,)), dma((7,)), dma((2,)),
        ],
        compiler_params=pltpu.CompilerParams(
            collective_id=0, has_side_effects=True, vmem_limit_bytes=48 << 20),
        name="ladder",
    )(*(pltpu.with_memory_space_constraint(a, pltpu.HBM) for a in (owner[None], targets.T, counts[None], amps, ints)))
    return out[:, :, None, :]


def solution(mesh):
    placed = (P("blk", "wide", None, None), P("wide", None, "blk", None), P(), P(), P())
    return jax.shard_map(
        body, mesh=mesh, in_specs=placed, out_specs=P(None, "blk", "wide", None), check_vma=False
    )
```

```python
import functools
import jax
import jax.numpy as jnp
from jax import lax
from jax.experimental import pallas as pl
from jax.experimental.pallas import tpu as pltpu
from jax.sharding import PartitionSpec as P

MESH = pl.DeviceIdType.MESH
NX, NY, NZ = 4, 4, 8
NW = NX * NZ
NI = 4
ROWS = NW * NI
GROUP = 4
PIECES = 4
GROUPS = NW // GROUP
ORDER = ((0, 0), (1, 0), (3, 0), (0, 1), (0, 7), (2, 0), (1, 1), (3, 1), (1, 7), (3, 7), (2, 1), (2, 7)) + tuple(
    (dx, dz) for dz in (4, 3, 5, 2, 6) for dx in range(4))
BLOCKS = ((0, 0, 4), (3, 0, 4), (1, 0, 4), (0, 4, 6), (0, 6, 8), (3, 4, 6), (1, 4, 6), (2, 0, 4),
          (3, 6, 8), (1, 6, 8), (2, 4, 6), (2, 6, 8))
SLOT = {}
for _part, _first, _end in BLOCKS:
    for _group in range(_first, _end):
        SLOT[_part, _group] = len(SLOT)
NT_DIMS = (((1,), (1,)), ((), ()))


def kernel(owner_hbm, targets_hbm, counts_hbm, amps_hbm, ints, out,
           owner, targets, counts, amps, stage, got, rows, held, turned, made, back, summed, final,
           arrive, from_up, from_down, far, home, last, local, sent, swap):
    w, b = lax.axis_index("wide"), lax.axis_index("blk")
    y, c = b // 2, b % 2
    xs = [lax.rem(w // NZ + d, NX) * NZ for d in range(NX)]
    zs = [lax.rem(w % NZ + d, NZ) for d in range(NZ)]
    blks = [lax.rem(y + d, NY) * 2 + c for d in range(NY)]

    def wide_at(step, sign):
        dx, dz = ORDER[step]
        return xs[sign * dx % NX] + zs[sign * dz % NZ]

    def remote(src, dst, send, recv, device):
        return pltpu.make_async_remote_copy(
            src_ref=src, dst_ref=dst, send_sem=send, recv_sem=recv,
            device_id=device, device_id_type=MESH)

    def await_bytes(ref, sem):
        pltpu.make_async_copy(ref, ref, sem).wait()

    partner = (w, y * 2 + 1 - c)

    loads = [pltpu.make_async_copy(src, dst, local.at[n]) for n, (src, dst) in enumerate((
        (amps_hbm, amps), (owner_hbm, owner), (targets_hbm, targets), (counts_hbm, counts), (ints, held.at[c])))]
    for load in loads:
        load.start()

    barrier = pltpu.get_barrier_semaphore()
    pl.semaphore_signal(barrier, inc=1, device_id=partner, device_id_type=MESH)
    for dy in (1, 3):
        pl.semaphore_signal(barrier, inc=1, device_id=(w, blks[dy]), device_id_type=MESH)
    for step in range(NW):
        for dy in (0, 2):
            if step or dy:
                pl.semaphore_signal(barrier, inc=1, device_id=(wide_at(step, 1), blks[dy]), device_id_type=MESH)

    for load in loads[:4]:
        load.wait()
    row = lax.broadcasted_iota(jnp.int32, (ROWS, ROWS), 0)
    col = lax.broadcasted_iota(jnp.int32, (ROWS, ROWS), 1)
    same = row % NI == col // NW

    def spread(value):
        return jnp.broadcast_to(jnp.concatenate([value] * NI, axis=1), (ROWS, ROWS))

    def one_hot(value):
        return jnp.where((spread(value) == row // NI) & same, 1.0, 0.0).astype(jnp.bfloat16)

    order = one_hot(owner[...])
    width = amps.shape[2]
    for j in range(4):
        lanes = slice(j * width // 4, (j + 1) * width // 4)
        piece = amps[:, :, lanes].reshape(ROWS, width // 4)
        value = jnp.dot(order, piece, preferred_element_type=jnp.float32).astype(jnp.bfloat16)
        stage[:, :, lanes] = value.reshape(NW, NI, width // 4)

    pl.semaphore_wait(barrier, 2 * NW + 2)

    mine = pltpu.make_async_copy(stage.at[w], got.at[0, 0], arrive.at[0])
    mine.start()
    for step in range(1, NW):
        to = wide_at(step, 1)
        for n in range(PIECES):
            lanes = pl.ds(n * (width // PIECES), width // PIECES)
            remote(stage.at[to, :, lanes], got.at[0, step, :, lanes], sent.at[0], arrive.at[step], (to, b)).start()

    exchange = remote(ints, held.at[c], swap.at[0], swap.at[1], partner)
    exchange.start()

    up, down = (w, blks[1]), (w, blks[NY - 1])
    pairs = held.shape[2]

    def lay(part, group):
        piece = got[part, group * GROUP:(group + 1) * GROUP].reshape(GROUP * NI, width)
        place = SLOT[part, group] * GROUP * NI
        rows[place:place + GROUP * NI, :] = piece

    def forward(group):
        for step in range(group * GROUP, (group + 1) * GROUP):
            chunk = got.at[0, step]
            await_bytes(chunk, arrive.at[step])
            remote(chunk, got.at[3, step], sent.at[1], from_down.at[step], up).start()
            remote(chunk, got.at[1, step], sent.at[2], from_up.at[step], down).start()
        lay(0, group)

    def relay(group):
        for step in range(group * GROUP, (group + 1) * GROUP):
            low, high = got.at[3, step], got.at[1, step]
            await_bytes(low, from_down.at[step])
            await_bytes(high, from_up.at[step])
            if step % 2 == 0:
                remote(low, got.at[2, step], sent.at[3], far.at[step], up).start()
            else:
                remote(high, got.at[2, step], sent.at[4], far.at[step], down).start()
        lay(3, group)
        lay(1, group)

    def finish(group):
        for step in range(group * GROUP, (group + 1) * GROUP):
            await_bytes(got.at[2, step], far.at[step])
        lay(2, group)

    def turn(core, k):
        lanes = pl.ds(pl.multiple_of((core * 2 + k) * pairs, pairs), pairs)
        turned[:, lanes] = held[core, k].T

    def contract(first, end, spare=0, lanes=(0, 1, 2, 3)):
        for n in lanes:
            cols = slice(n * pairs, (n + 1) * pairs)
            value = jnp.dot(rows[first - spare:end, :], turned[:, cols], preferred_element_type=jnp.float32)[spare:]
            made[first // NI:end // NI, :, cols] = value.astype(jnp.bfloat16).reshape((end - first) // NI, NI, pairs)

    def give(part, first, end, lanes=slice(None)):
        for step in range(first * GROUP, end * GROUP):
            chunk = made.at[SLOT[part, step // GROUP] * GROUP + step % GROUP, :, lanes]
            there = back.at[part, w, :, lanes]
            if part == 2:
                remote(chunk, there, sent.at[5], home.at[part], (wide_at(step, -1), blks[2])).start()
            elif step == 0:
                pltpu.make_async_copy(chunk, there, home.at[part]).start()
            else:
                remote(chunk, there, sent.at[5], home.at[part], (wide_at(step, -1), b)).start()

    def sumup(part):
        await_bytes(back.at[part], home.at[part])
        piece = back[part].reshape(ROWS, 4 * pairs)
        for cc in range(2):
            total = jnp.dot(pick[0], piece[:, 2 * cc * pairs:(2 * cc + 1) * pairs], preferred_element_type=jnp.float32)
            total += jnp.dot(pick[1], piece[:, (2 * cc + 1) * pairs:(2 * cc + 2) * pairs], preferred_element_type=jnp.float32)
            total = total.astype(jnp.bfloat16).reshape(NW, NI, pairs)
            if part % 2 == 0:
                origin = lax.rem(y + part, NY)
                out[:, :, pl.ds(pl.multiple_of((origin * 2 + cc) * pairs, pairs), pairs)] = total
            else:
                summed[part, :, :, cc * pairs:(cc + 1) * pairs] = total
        if part % 2:
            remote(summed.at[part], final.at[part], sent.at[6], last.at[part], (w, blks[part])).start()

    def settle(part):
        await_bytes(final.at[part], last.at[part])
        origin = lax.rem(y + NY - part, NY)
        out[:, :, pl.ds(pl.multiple_of(origin * 2 * pairs, 2 * pairs), 2 * pairs)] = final[part]

    forward(0)
    loads[4].wait()
    turn(c, 0)
    forward(1)
    turn(c, 1)
    forward(2)
    relay(0)

    pick = []
    for k in range(2):
        live = jnp.where(counts[...] > k, targets[k:k + 1, :], -1)
        chosen = lax.dot_general(one_hot(live), order, NT_DIMS, preferred_element_type=jnp.float32)
        pick.append(chosen.astype(jnp.bfloat16))

    exchange.wait_recv()
    turn(1 - c, 0)
    forward(3)
    relay(1)
    turn(1 - c, 1)
    contract(0, 64)
    give(0, 0, 4)
    forward(4)
    relay(2)
    finish(0)
    forward(5)
    relay(3)
    finish(1)
    contract(64, 224)
    give(3, 0, 4)
    give(1, 0, 4)
    give(0, 4, 6)
    forward(6)
    relay(4)
    finish(2)
    forward(7)
    relay(5)
    finish(3)
    contract(224, 384)
    give(3, 4, 6)
    give(1, 4, 6)
    give(0, 6, 8)
    relay(6)
    relay(7)
    contract(384, 448, 64)
    give(3, 6, 8)
    give(1, 6, 8)
    give(2, 0, 4)
    finish(4)
    finish(5)
    contract(448, 480, 96)
    give(2, 4, 6)
    finish(6)
    finish(7)
    for cc in range(2):
        contract(480, 512, 96, (2 * cc, 2 * cc + 1))
        give(2, 6, 8, pl.ds(2 * cc * pairs, 2 * pairs))

    sumup(3)
    sumup(1)
    sumup(0)
    sumup(2)
    settle(3)
    settle(1)

    await_bytes(stage.at[pl.ds(0, NW - 1)], sent.at[0])
    await_bytes(got.at[0], sent.at[1])
    await_bytes(got.at[0], sent.at[2])
    await_bytes(got.at[2, pl.ds(0, NW // 2)], sent.at[3])
    await_bytes(got.at[2, pl.ds(0, NW // 2)], sent.at[4])
    await_bytes(made.at[pl.ds(0, NY * NW - 3)], sent.at[5])
    await_bytes(summed.at[pl.ds(0, 2)], sent.at[6])
    exchange.wait_send()


def body(amplitudes, integrals, owner, targets, counts):
    amps, ints = amplitudes[:, 0], integrals[0]
    width = amps.shape[2]
    pairs = ints.shape[1]
    dma = pltpu.SemaphoreType.DMA
    out = pl.pallas_call(
        kernel,
        out_shape=jax.ShapeDtypeStruct((NW, NI, 2 * NY * pairs), jnp.bfloat16),
        in_specs=[pl.BlockSpec(memory_space=pltpu.HBM)] * 5,
        out_specs=pl.BlockSpec(memory_space=pltpu.VMEM),
        scratch_shapes=[
            pltpu.VMEM((1, NW), jnp.int32),
            pltpu.VMEM((2, NW), jnp.int32),
            pltpu.VMEM((1, NW), jnp.int32),
            pltpu.VMEM((NI, NW, width), jnp.bfloat16),
            pltpu.VMEM((NW, NI, width), jnp.bfloat16),
            pltpu.VMEM((NY, NW, NI, width), jnp.bfloat16),
            pltpu.VMEM((NY * ROWS, width), jnp.bfloat16),
            pltpu.VMEM((2, 2, pairs, width), jnp.bfloat16),
            pltpu.VMEM((width, 4 * pairs), jnp.bfloat16),
            pltpu.VMEM((NY * NW, NI, 4 * pairs), jnp.bfloat16),
            pltpu.VMEM((NY, NW, NI, 4 * pairs), jnp.bfloat16),
            pltpu.VMEM((NY, NW, NI, 2 * pairs), jnp.bfloat16),
            pltpu.VMEM((NY, NW, NI, 2 * pairs), jnp.bfloat16),
            dma((NW,)), dma((NW,)), dma((NW,)), dma((NW,)), dma((NY,)), dma((NY,)), dma((5,)), dma((7,)), dma((2,)),
        ],
        compiler_params=pltpu.CompilerParams(
            collective_id=0, has_side_effects=True, vmem_limit_bytes=48 << 20),
        name="ladder",
    )(*(pltpu.with_memory_space_constraint(a, pltpu.HBM) for a in (owner[None], targets.T, counts[None], amps, ints)))
    return out[:, :, None, :]


def solution(mesh):
    placed = (P("blk", "wide", None, None), P("wide", None, "blk", None), P(), P(), P())
    return jax.shard_map(
        body, mesh=mesh, in_specs=placed, out_specs=P(None, "blk", "wide", None), check_vma=False
    )
```
